32 devices in a mesh: inl: 4 (over x, core), xl: 8 (over z, y).
Axes of the slice: x: 2, y: 2, z: 4, core: 2. Of those that a mesh axis runs over, the one named last changes fastest.
Arguments:
- baseline: float32 [16, 128, 1024], P('inl', 'xl'), may hold values from -600 to 600
- monitor: float32 [16, 128, 1024], P('inl', 'xl'), may hold values from -900 to 900
- shift_model: float32 [4, 32, 128], P(None, None, 'xl'), may hold values from -4 to 4
- knot_start: int32 [32, 4], replicated, may hold values from -12 to 13, as said below
- half_width: int32 [8], P('xl'), may hold values from 1 to 3
Outputs:
- shift_obs: float32 [16, 128, 1024], P('inl', 'xl')
- delta: float32 [4, 32, 128], P(None, 'xl', 'inl')
The draws below stay inside these ranges and needn't reach their ends.
Inputs may be any that keep to these rules, and one draw needn't show every extreme that they name: `knot_start`: basis function k of a window starts at sample k * 8 - 3 * 4 or one later, relative to the window's first sample.
All inputs are finite; a program needn't handle non-finite values.
Results may differ from the reference program's by a relative error of at most 0.00018.
Values sent between devices are 32-bit elements; how exact they have to be, the bound alone decides.
A program may use at most 64 MiB of HBM per device.

```python
import math
import jax
import jax.numpy as jnp
from jax import lax

NT = 1024
LAGS = 15
TWIN = 12
HMAX = 3
WINLEN = 32
KW = 4
KSTEP = 8
XL_DEV = 16
NIL = 16
NXL = 128
NWIN = 32
SLABS = 8


def make_pair(key):
    base_key = jax.random.fold_in(key, 4242)
    key_raw = jax.random.fold_in(base_key, 1)
    key_lag = jax.random.fold_in(base_key, 2)
    key_trace = jax.random.fold_in(base_key, 3)
    key_envelope = jax.random.fold_in(base_key, 4)
    key_noise = jax.random.fold_in(base_key, 5)
    raw = jnp.clip(jax.random.normal(key_raw, (NIL, NXL, NT + 2 * LAGS), jnp.float32), -6.0, 6.0)
    noise = 0.5 * jnp.clip(jax.random.normal(key_noise, (NIL, NXL, NT), jnp.float32), -6.0, 6.0)
    lagging = jax.random.randint(key_lag, (NIL, NXL, 1), -7, 8)
    index_at = jnp.arange(NT)[None, None, :] + LAGS + lagging
    shifted = jnp.take_along_axis(raw, index_at, 2)
    drawn = raw[:, :, LAGS:LAGS + NT]
    trace_scale = jnp.exp(jax.random.uniform(key_trace, (NIL, NXL, 1), jnp.float32, 0.0, math.log(10.0)))
    blocks = jnp.exp(jax.random.uniform(key_envelope, (NIL, NXL, NT // 64), jnp.float32, 0.0, math.log(10.0)))
    envelope = jnp.repeat(blocks, 64, axis=2) * trace_scale / 10.0 * 10.0
    scaled = jnp.minimum(envelope, 100.0)
    return (drawn * scaled, (shifted + noise) * scaled)


def draw_baseline(key, part):
    return make_pair(key)[0]


def draw_monitor(key, part):
    return make_pair(key)[1]


def draw_knot_start(key, part):
    key_jitter = jax.random.fold_in(key, 77)
    jitter = jax.random.randint(key_jitter, (NWIN, KW), 0, 2)
    lowest = 0 - 3 * KSTEP // 2
    starts = KSTEP * jnp.arange(KW)[None, :] + lowest + jitter
    starts = starts.at[0, 0].set(lowest)
    starts = starts.at[0, KW - 1].set(KSTEP * (KW - 1) + lowest + 1)
    return starts.astype(jnp.int32)


def draw_half_width(key, part):
    key_values = jax.random.fold_in(key, 91)
    key_place = jax.random.fold_in(key, 92)
    widths = jax.random.randint(key_values, (SLABS,), 1, HMAX + 1)
    largest = jax.random.randint(key_place, (), 0, SLABS)
    widths = widths.at[largest].set(HMAX)
    widths = widths.at[(largest + 1) % SLABS].set(1)
    return widths.astype(jnp.int32)


def level_of(stream_key, extent, shards, low, high):
    def one(axis_at, shards_of):
        heights = jax.random.uniform(jax.random.fold_in(jax.random.fold_in(stream_key, 6), axis_at), (shards_of,), jnp.float32, low / len(shards), high / len(shards))
        return jnp.repeat(jnp.exp(heights), extent[axis_at] // shards_of).reshape((-1,) + (1,) * (len(extent) - axis_at - 1))

    gain = one(*shards[0])
    for cut in shards[1:]:
        gain = gain * one(*cut)
    return gain


def scatter_about(rng, dims, deviation, most, shards=(), held_as=jnp.bfloat16):
    values = jax.random.normal(rng, dims, jnp.float32) * deviation
    if len(shards) > 0:
        values = level_of(rng, dims, shards, -0.22, 0.18) * values
    return jnp.clip(values, min=-most, max=most).astype(held_as)


def setup_inputs(seed: int = 0) -> dict:
    key_of = jax.random.split(jax.random.key(seed), 6)
    return {
        "baseline": draw_baseline(jax.random.fold_in(key_of[5], 71), 0),
        "monitor": draw_monitor(jax.random.fold_in(key_of[5], 71), 0),
        "shift_model": scatter_about(key_of[2], (KW, NWIN, NXL), 1.0, 4.0, ((2, 8),), jnp.float32),
        "knot_start": draw_knot_start(jax.random.fold_in(key_of[5], 71), 0),
        "half_width": draw_half_width(jax.random.fold_in(key_of[5], 71), 0),
    }


EPSILON = 1e-06
SHARPNESS = 6.0
DAMPING = 0.5

def spline(offset):
    square = offset * offset
    cubed = square * offset
    piece_one = cubed / 6.0
    piece_two = (-3.0 * cubed + 12.0 * square - 12.0 * offset + 4.0) / 6.0
    piece_three = (3.0 * cubed - 24.0 * square + 60.0 * offset - 44.0) / 6.0
    remain = 4.0 - offset
    piece_four = remain * remain * remain / 6.0
    result = jnp.where(offset < 4.0, piece_four, 0.0 * offset)
    result = jnp.where(offset < 3.0, piece_three, result)
    result = jnp.where(offset < 2.0, piece_two, result)
    result = jnp.where(offset < 1.0, piece_one, result)
    return jnp.where(offset < 0.0, 0.0 * offset, result)

def basis_table(knot_start):
    positions = jnp.arange(WINLEN).astype(jnp.float32)
    offset = (positions[None, None, :] - knot_start[:, :, None].astype(jnp.float32)) / KSTEP
    return spline(offset)

def solve_small(matrix, target):
    lower = [[None] * KW for _ in range(KW)]
    for column in range(KW):
        pivot = matrix[column][column]
        for inner in range(column):
            pivot = pivot - lower[column][inner] * lower[column][inner]
        lower[column][column] = jnp.sqrt(pivot)
        for target_row in range(column + 1, KW):
            entry = matrix[target_row][column]
            for inner in range(column):
                entry = entry - lower[target_row][inner] * lower[column][inner]
            lower[target_row][column] = entry / lower[column][column]
    forward = []
    for column in range(KW):
        entry = target[column]
        for inner in range(column):
            entry = entry - lower[column][inner] * forward[inner]
        forward.append(entry / lower[column][column])
    backward = [None] * KW
    for column in range(KW - 1, -1, -1):
        entry = forward[column]
        for inner in range(column + 1, KW):
            entry = entry - lower[inner][column] * backward[inner]
        backward[column] = entry / lower[column][column]
    return jnp.stack(backward)

def box_time(values):
    samples = values.shape[2]
    width = 2 * TWIN + 1
    padded = jnp.pad(values, ((0, 0), (0, 0), (TWIN, TWIN)))
    partial_sums = {1: padded}
    length = 1
    while 2 * length <= width:
        previous = partial_sums[length]
        partial_sums[2 * length] = previous[:, :, :-length] + previous[:, :, length:]
        length = 2 * length
    total = None
    begin = 0
    remain = width
    while remain > 0:
        if length <= remain:
            piece = partial_sums[length][:, :, begin:begin + samples]
            total = piece if total is None else total + piece
            begin = begin + length
            remain = remain - length
        length = length // 2
    return total

def smooth(values, widths):
    timed = box_time(values)
    crossl = values.shape[1]
    sided = jnp.pad(timed, ((0, 0), (HMAX, HMAX), (0, 0)))
    total = None
    for offset in range(-HMAX, HMAX + 1):
        weight = (jnp.abs(offset) <= widths).astype(jnp.float32)[None, :, None]
        term = weight * sided[:, HMAX + offset:HMAX + offset + crossl]
        total = term if total is None else total + term
    return total

def reference(baseline, monitor, shift_model, knot_start, half_width):
    widths = jnp.repeat(half_width, XL_DEV)
    energy_base = smooth(baseline * baseline, widths)
    moni_pad = jnp.pad(monitor, ((0, 0), (0, 0), (LAGS, LAGS)))
    energy_mon = smooth(moni_pad * moni_pad, widths)
    total_exp = None
    for lag_value in range(-LAGS, LAGS + 1):
        lagged = moni_pad[:, :, LAGS + lag_value:LAGS + lag_value + NT]
        correlation = smooth(baseline * lagged, widths)
        energy = energy_mon[:, :, LAGS + lag_value:LAGS + lag_value + NT]
        normed = correlation / jnp.sqrt(energy_base * energy + EPSILON)
        weight_exp = jnp.exp(SHARPNESS * normed)
        if total_exp is None:
            total_exp = weight_exp
            total_shift = lag_value * weight_exp
            total_corr = normed * weight_exp
        else:
            total_exp = total_exp + weight_exp
            total_shift = total_shift + lag_value * weight_exp
            total_corr = total_corr + normed * weight_exp
    shift_obs = total_shift / total_exp
    confidence = 0.5 + 0.5 * total_corr / total_exp
    table = basis_table(knot_start)
    modelled = jnp.einsum('kwx,wku->xwu', shift_model, table, precision=lax.Precision.HIGHEST).reshape(NXL, NT)
    resid = shift_obs - modelled[None]
    resid_four = resid.reshape(NIL, NXL, NWIN, WINLEN)
    conf_four = confidence.reshape(NIL, NXL, NWIN, WINLEN)
    grad = jnp.einsum('ixwu,wku->kwx', conf_four * resid_four, table, precision=lax.Precision.HIGHEST)
    hess = jnp.einsum('ixwu,wku,wju->kjwx', conf_four, table, table, precision=lax.Precision.HIGHEST)
    matrix = [[hess[first_k, second_k] + (DAMPING * NIL if first_k == second_k else 0.0) for second_k in range(KW)] for first_k in range(KW)]
    target = [grad[first_k] for first_k in range(KW)]
    delta = solve_small(matrix, target)
    return (shift_obs, delta)
```

```python
import functools
import math

import jax
import jax.numpy as jnp
from jax import lax
from jax.experimental import pallas as pl
from jax.experimental.pallas import tpu as pltpu
from jax.sharding import PartitionSpec as P

LAGS = 15
TWIN = 12
HMAX = 3
WINLEN = 32
KW = 4
KSTEP = 8
EPSILON = 1e-06
SHARPNESS = 6.0
DAMPING = 0.5

LANES = 128
SUB = 8
REACH = LAGS + TWIN
PAIRS = [(k, j) for k in range(KW) for j in range(k + 1)]
TERMS = KW + len(PAIRS)
MESH_ID = pl.DeviceIdType.MESH


def spline(offset):
    square = offset * offset
    cubed = square * offset
    piece_one = cubed / 6.0
    piece_two = (-3.0 * cubed + 12.0 * square - 12.0 * offset + 4.0) / 6.0
    piece_three = (3.0 * cubed - 24.0 * square + 60.0 * offset - 44.0) / 6.0
    remain = 4.0 - offset
    piece_four = remain * remain * remain / 6.0
    result = jnp.where(offset < 4.0, piece_four, 0.0 * offset)
    result = jnp.where(offset < 3.0, piece_three, result)
    result = jnp.where(offset < 2.0, piece_two, result)
    result = jnp.where(offset < 1.0, piece_one, result)
    return jnp.where(offset < 0.0, 0.0 * offset, result)


def box_sums(term, count, put):
    outs = -(-count // SUB)
    terms = {}

    def block(number):
        if number not in terms:
            terms[number] = [term(number * SUB + j) for j in range(SUB)]
        return terms[number]

    totals = {}
    suffixes = {}

    def total(number):
        if number not in totals:
            vals = block(number)
            while len(vals) > 1:
                vals = [vals[2 * j] + vals[2 * j + 1] for j in range(len(vals) // 2)]
            totals[number] = vals[0]
        return totals[number]

    def suffix(number):
        if number not in suffixes:
            vals = list(block(number))
            for j in range(SUB - 2, -1, -1):
                vals[j] = vals[j] + vals[j + 1]
            suffixes[number] = vals
            totals[number] = vals[0]
        return suffixes[number]

    for number in range(outs):
        tail = suffix(number)
        if number + 1 < outs:
            suffix(number + 1)
        if number + 2 < outs:
            suffix(number + 2)
        run = total(number + 1) + total(number + 2)
        for j in range(SUB):
            if number * SUB + j < count:
                position = (number + 3) * SUB + j
                if number + 3 in terms:
                    value = terms[number + 3][j]
                elif number + 3 < outs + 2:
                    value = block(number + 3)[j]
                else:
                    value = term(position)
                run = run + value
                put(number * SUB + j, tail[j] + run)


def main_kernel(
    half_ref, pair_ref, model_ref, knot_ref, shift_ref, normal_ref,
    base, moni, timed, ebase, emoni, texp, tshift, tcorr, phi, flat,
):
    width = ebase.shape[1]
    rows = base.shape[1]
    half = half_ref[0]
    take_two = (half >= 2).astype(jnp.float32)
    take_three = (half >= 3).astype(jnp.float32)
    lane = lax.broadcasted_iota(jnp.int32, (rows, LANES), 1) % WINLEN
    has_before = (lane != 0).astype(jnp.float32)
    has_after = (lane != WINLEN - 1).astype(jnp.float32)

    for which, (ref, halo) in enumerate(((base, TWIN), (moni, REACH))):
        for u in range(WINLEN):
            value = pair_ref[which, u]
            ref[halo + u] = value
            if u >= WINLEN - halo:
                ref[halo + u - WINLEN] = pltpu.roll(value, 1, 1) * has_before
            if u < halo:
                ref[halo + u + WINLEN] = pltpu.roll(value, LANES - 1, 1) * has_after

    def smooth(term, count, put):
        for part in range(rows // SUB):
            band = pl.ds(part * SUB, SUB)

            def keep(r, value, band=band):
                timed[r, band, :] = value

            box_sums(lambda r, band=band: term(r, band), count, keep)
        for r in range(count):
            for part in range(width // SUB):
                near = [timed[r, pl.ds(part * SUB + d, SUB), :] for d in range(2 * HMAX + 1)]
                value = near[3] + (near[2] + near[4])
                value = value + take_two * (near[1] + near[5])
                value = value + take_three * (near[0] + near[6])
                put(r, pl.ds(part * SUB, SUB), value)

    def base_square(r, band):
        value = base[r, band, :]
        return value * value

    def put_base(r, band, value):
        ebase[r, band, :] = value

    smooth(base_square, WINLEN, put_base)

    def moni_square(r, band):
        value = moni[r, band, :]
        return value * value

    def put_moni(r, band, value):
        emoni[r, band, :] = value

    smooth(moni_square, WINLEN + 2 * LAGS, put_moni)

    texp[...] = jnp.zeros_like(texp)
    tshift[...] = jnp.zeros_like(tshift)
    tcorr[...] = jnp.zeros_like(tcorr)

    @pl.loop(0, 2 * LAGS + 1)
    def _(lag):
        lag_value = (lag - LAGS).astype(jnp.float32)

        def product(r, band):
            return base[r, band, :] * moni[lag + r, band, :]

        def finish(r, band, value):
            energy = ebase[r, band, :] * emoni[lag + r, band, :] + EPSILON
            normed = value * lax.rsqrt(energy)
            weight = jnp.exp2(normed * (SHARPNESS * math.log2(math.e)))
            texp[r, band, :] += weight
            tshift[r, band, :] += lag_value * weight
            tcorr[r, band, :] += normed * weight

        smooth(product, WINLEN, finish)

    sample = lax.broadcasted_iota(jnp.int32, (WINLEN, LANES), 0).astype(jnp.float32)
    for k in range(KW):
        start = knot_ref[pl.ds(k, 1), :].astype(jnp.float32)
        phi[k] = spline((sample - start) / KSTEP)

    for part in range(width // SUB):
        band = pl.ds(part * SUB, SUB)
        sums = [jnp.zeros((SUB, LANES), jnp.float32)] * TERMS
        for u in range(WINLEN):
            inverse = 1.0 / texp[u, band, :]
            observed = tshift[u, band, :] * inverse
            shift_ref[u, band, :] = observed
            conf = 0.5 + 0.5 * (tcorr[u, band, :] * inverse)
            basis = [phi[k, pl.ds(u, 1), :] for k in range(KW)]
            tau = model_ref[0, band, :] * basis[0]
            for k in range(1, KW):
                tau = tau + model_ref[k, band, :] * basis[k]
            weighted = conf * (observed - tau)
            for k in range(KW):
                sums[k] = sums[k] + weighted * basis[k]
            for place, (k, j) in enumerate(PAIRS):
                sums[KW + place] = sums[KW + place] + conf * (basis[k] * basis[j])
        for place in range(TERMS):
            value = sums[place]
            value = value + pltpu.roll(value, 2 * WINLEN, 1)
            value = value + pltpu.roll(value, WINLEN, 1)
            flat[pl.ds(place * width + part * SUB, SUB), :] = value
    spare = flat.shape[0] - TERMS * width
    if spare:
        flat[pl.ds(TERMS * width, spare), :] = jnp.zeros((spare, LANES), jnp.float32)
    turned = flat[...].T
    owners, share = normal_ref.shape[0], normal_ref.shape[1]
    for owner in range(owners):
        normal_ref[owner] = turned[owner * share : (owner + 1) * share]


def solve_small(matrix, target):
    lower = [[None] * KW for _ in range(KW)]
    for column in range(KW):
        pivot = matrix[column][column]
        for inner in range(column):
            pivot = pivot - lower[column][inner] * lower[column][inner]
        lower[column][column] = jnp.sqrt(pivot)
        for target_row in range(column + 1, KW):
            entry = matrix[target_row][column]
            for inner in range(column):
                entry = entry - lower[target_row][inner] * lower[column][inner]
            lower[target_row][column] = entry / lower[column][column]
    forward = []
    for column in range(KW):
        entry = target[column]
        for inner in range(column):
            entry = entry - lower[column][inner] * forward[inner]
        forward.append(entry / lower[column][column])
    backward = [None] * KW
    for column in range(KW - 1, -1, -1):
        entry = forward[column]
        for inner in range(column + 1, KW):
            entry = entry - lower[inner][column] * backward[inner]
        backward[column] = entry / lower[column][column]
    return backward


def owner_kernel(groups, slabs, width, damping, mine_ref, out_ref, held, send_sem, recv_sem):
    row, col = lax.axis_index("inl"), lax.axis_index("xl")
    each = slabs // groups
    target_row = col // each
    place = row * each + col % each
    barrier = pltpu.get_barrier_semaphore()
    for step in range(slabs):
        source_row, source_col = step // each, row * each + step % each

        @pl.when(jnp.logical_or(source_row != row, source_col != col))
        def _():
            pl.semaphore_signal(
                barrier, inc=1, device_id=(source_row, source_col), device_id_type=MESH_ID
            )

    @pl.when(target_row == row)
    def _():
        pl.semaphore_wait(barrier, slabs - 1)

    @pl.when(target_row != row)
    def _():
        pl.semaphore_wait(barrier, slabs)

    def send(step):
        return pltpu.make_async_remote_copy(
            src_ref=mine_ref.at[step],
            dst_ref=held.at[place],
            send_sem=send_sem.at[step],
            recv_sem=recv_sem.at[place],
            device_id=(target_row, step),
            device_id_type=MESH_ID,
        )

    def local():
        return pltpu.make_async_copy(mine_ref.at[col], held.at[place], recv_sem.at[place])

    for step in range(slabs):
        self_copy = jnp.logical_and(target_row == row, col == step)

        @pl.when(self_copy)
        def _():
            local().start()

        @pl.when(jnp.logical_not(self_copy))
        def _():
            send(step).start()

    for step in range(slabs):
        pltpu.make_async_copy(mine_ref.at[0], held.at[step], recv_sem.at[step]).wait()

    share = held.shape[1]
    for part in range(each):
        total = held[part]
        for group in range(1, groups):
            total = total + held[group * each + part]

        def term(number):
            return total[:, number * width : (number + 1) * width]

        matrix = [[None] * KW for _ in range(KW)]
        for number, (k, j) in enumerate(PAIRS):
            matrix[k][j] = term(KW + number) + (damping if k == j else 0.0)
        delta = solve_small(matrix, [term(k) for k in range(KW)])
        for k in range(KW):
            out_ref[k, :, pl.ds(part * width, width)] = delta[k]

    for step in range(slabs):
        self_copy = jnp.logical_and(target_row == row, col == step)

        @pl.when(jnp.logical_not(self_copy))
        def _():
            send(step).wait_send()


def extended(block, axis, dim, width):
    count = lax.axis_size(axis)
    forward = [(i, i + 1) for i in range(count - 1)]
    backward = [(target, source) for source, target in forward]
    low = lax.ppermute(
        lax.slice_in_dim(block, block.shape[dim] - width, None, axis=dim), axis, forward
    )
    high = lax.ppermute(lax.slice_in_dim(block, 0, width, axis=dim), axis, backward)
    return jnp.concatenate([low, block, high], axis=dim)


def per_device(baseline, monitor, shift_model, knot_start, half_width):
    inline_rows, width, samples = baseline.shape
    windows = samples // WINLEN
    groups, slabs = lax.axis_size("inl"), lax.axis_size("xl")
    share = windows // slabs
    rows = -(-(width + 2 * HMAX) // SUB) * SUB
    paired = extended(jnp.stack([baseline, monitor]), "xl", 2, HMAX)
    paired = jnp.pad(paired, ((0, 0), (0, 0), (0, rows - width - 2 * HMAX), (0, 0)))
    pair = paired.reshape(2, inline_rows, rows, windows, WINLEN)
    pair = pair.transpose(0, 4, 2, 1, 3).reshape(2, WINLEN, rows, LANES)
    model = jnp.tile(shift_model.transpose(0, 2, 1), (1, 1, inline_rows))
    knots = jnp.tile(knot_start.T, (1, inline_rows))
    packed = -(-(TERMS * width) // LANES) * LANES
    block = (WINLEN, width, LANES)
    f32 = jnp.float32
    whole = pl.BlockSpec(memory_space=pltpu.VMEM)
    shift, normal = pl.pallas_call(
        main_kernel,
        out_shape=(
            jax.ShapeDtypeStruct(block, f32),
            jax.ShapeDtypeStruct((slabs, share, packed), f32),
        ),
        in_specs=[pl.BlockSpec(memory_space=pltpu.SMEM), whole, whole, whole],
        out_specs=(whole, whole),
        scratch_shapes=[
            pltpu.VMEM((WINLEN + 2 * TWIN, rows, LANES), f32),
            pltpu.VMEM((WINLEN + 2 * REACH + 2, rows, LANES), f32),
            pltpu.VMEM((WINLEN + 2 * LAGS, rows, LANES), f32),
            pltpu.VMEM(block, f32),
            pltpu.VMEM((WINLEN + 2 * LAGS, width, LANES), f32),
            pltpu.VMEM(block, f32),
            pltpu.VMEM(block, f32),
            pltpu.VMEM(block, f32),
            pltpu.VMEM((KW, WINLEN, LANES), f32),
            pltpu.VMEM((packed, LANES), f32),
        ],
        compiler_params=pltpu.CompilerParams(vmem_limit_bytes=32 * 1024 * 1024),
        name="lags",
    )(half_width, pair, model, knots)
    shift_obs = shift.reshape(WINLEN, width, inline_rows, windows)
    shift_obs = shift_obs.transpose(2, 1, 3, 0).reshape(inline_rows, width, samples)
    each = slabs // groups
    delta = pl.pallas_call(
        functools.partial(owner_kernel, groups, slabs, width, DAMPING * inline_rows * groups),
        out_shape=jax.ShapeDtypeStruct((KW, share, each * width), f32),
        in_specs=[whole],
        out_specs=whole,
        scratch_shapes=[
            pltpu.VMEM((slabs, share, packed), f32),
            pltpu.SemaphoreType.DMA((slabs,)),
            pltpu.SemaphoreType.DMA((slabs,)),
        ],
        compiler_params=pltpu.CompilerParams(collective_id=0, has_side_effects=True),
        name="owners",
    )(normal)
    return (shift_obs, delta)


def solution(mesh):
    in_specs = (P("inl", "xl", None), P("inl", "xl", None), P(None, None, "xl"), P(), P("xl"))
    out_specs = (P("inl", "xl", None), P(None, "xl", "inl"))
    return jax.shard_map(
        per_device, mesh=mesh, in_specs=in_specs, out_specs=out_specs, check_vma=False
    )
```

```python
import functools
import math

import jax
import jax.numpy as jnp
from jax import lax
from jax.experimental import pallas as pl
from jax.experimental.pallas import tpu as pltpu
from jax.sharding import PartitionSpec as P

LAGS = 15
TWIN = 12
HMAX = 3
WINLEN = 32
KW = 4
KSTEP = 8
EPSILON = 1e-06
SHARPNESS = 6.0
DAMPING = 0.5

LANES = 128
SUB = 8
REACH = LAGS + TWIN
PAIRS = [(k, j) for k in range(KW) for j in range(k + 1)]
TERMS = KW + len(PAIRS)
MESH_ID = pl.DeviceIdType.MESH


def spline(offset):
    square = offset * offset
    cubed = square * offset
    piece_one = cubed / 6.0
    piece_two = (-3.0 * cubed + 12.0 * square - 12.0 * offset + 4.0) / 6.0
    piece_three = (3.0 * cubed - 24.0 * square + 60.0 * offset - 44.0) / 6.0
    remain = 4.0 - offset
    piece_four = remain * remain * remain / 6.0
    result = jnp.where(offset < 4.0, piece_four, 0.0 * offset)
    result = jnp.where(offset < 3.0, piece_three, result)
    result = jnp.where(offset < 2.0, piece_two, result)
    result = jnp.where(offset < 1.0, piece_one, result)
    return jnp.where(offset < 0.0, 0.0 * offset, result)


def box_sums(term, count, put):
    outs = -(-count // SUB)
    terms = {}

    def block(number):
        if number not in terms:
            terms[number] = [term(number * SUB + j) for j in range(SUB)]
        return terms[number]

    totals = {}
    suffixes = {}

    def total(number):
        if number not in totals:
            vals = block(number)
            while len(vals) > 1:
                vals = [vals[2 * j] + vals[2 * j + 1] for j in range(len(vals) // 2)]
            totals[number] = vals[0]
        return totals[number]

    def suffix(number):
        if number not in suffixes:
            vals = list(block(number))
            for j in range(SUB - 2, -1, -1):
                vals[j] = vals[j] + vals[j + 1]
            suffixes[number] = vals
            totals[number] = vals[0]
        return suffixes[number]

    for number in range(outs):
        tail = suffix(number)
        if number + 1 < outs:
            suffix(number + 1)
        if number + 2 < outs:
            suffix(number + 2)
        run = total(number + 1) + total(number + 2)
        for j in range(SUB):
            if number * SUB + j < count:
                position = (number + 3) * SUB + j
                if number + 3 in terms:
                    value = terms[number + 3][j]
                elif number + 3 < outs + 2:
                    value = block(number + 3)[j]
                else:
                    value = term(position)
                run = run + value
                put(number * SUB + j, tail[j] + run)


def trace_rows(i, x, width):
    return pl.ds((i * (width // SUB) + x // SUB) * SUB * SUB + x % SUB, SUB, stride=SUB)


def edge_tile(which, j, i, lines):
    return pl.ds(((which * HMAX + j) * lines + i) * SUB, SUB)


def swap_blocks(parts):
    block = lax.broadcasted_iota(jnp.int32, parts[0].shape, 1) // WINLEN
    low, even = block < 2, block % 2 == 0
    w, x, y, z = parts
    w, y = jnp.where(low, w, pltpu.roll(y, 64, 1)), jnp.where(low, pltpu.roll(w, 64, 1), y)
    x, z = jnp.where(low, x, pltpu.roll(z, 64, 1)), jnp.where(low, pltpu.roll(x, 64, 1), z)
    w, x = jnp.where(even, w, pltpu.roll(x, 32, 1)), jnp.where(even, pltpu.roll(w, 96, 1), x)
    y, z = jnp.where(even, y, pltpu.roll(z, 32, 1)), jnp.where(even, pltpu.roll(y, 96, 1), z)
    return [w, x, y, z]


def halo_kernel(width, base_ref, moni_ref, out_ref, edge, held, send_sem, recv_sem):
    row, col = lax.axis_index("inl"), lax.axis_index("xl")
    last = lax.axis_size("xl") - 1
    lines = base_ref.shape[0] // (width * SUB)
    barrier = pltpu.get_barrier_semaphore()
    has_left, has_right = col > 0, col < last

    @pl.when(has_left)
    def _():
        pl.semaphore_signal(barrier, inc=1, device_id=(row, col - 1), device_id_type=MESH_ID)

    @pl.when(has_right)
    def _():
        pl.semaphore_signal(barrier, inc=1, device_id=(row, col + 1), device_id_type=MESH_ID)

    for side, first in ((0, width - HMAX), (1, 0)):
        for which, ref in enumerate((base_ref, moni_ref)):
            for j in range(HMAX):
                for i in range(lines):
                    value = ref[trace_rows(i, first + j, width), :]
                    edge[side, edge_tile(which, j, i, lines), :] = value

    @pl.when(jnp.logical_and(has_left, has_right))
    def _():
        pl.semaphore_wait(barrier, 2)

    @pl.when(jnp.logical_not(jnp.logical_and(has_left, has_right)))
    def _():
        pl.semaphore_wait(barrier, 1)

    def copy(side, target):
        return pltpu.make_async_remote_copy(
            src_ref=edge.at[side],
            dst_ref=held.at[side],
            send_sem=send_sem.at[side],
            recv_sem=recv_sem.at[side],
            device_id=(row, target),
            device_id_type=MESH_ID,
        )

    @pl.when(has_right)
    def _():
        copy(0, col + 1).start()

    @pl.when(has_left)
    def _():
        copy(1, col - 1).start()

    @pl.when(has_left)
    def _():
        pltpu.make_async_copy(edge.at[0], held.at[0], recv_sem.at[0]).wait()
        out_ref[0] = held[0]

    @pl.when(jnp.logical_not(has_left))
    def _():
        out_ref[0] = jnp.zeros(out_ref.shape[1:], jnp.float32)

    @pl.when(has_right)
    def _():
        pltpu.make_async_copy(edge.at[1], held.at[1], recv_sem.at[1]).wait()
        out_ref[1] = held[1]

    @pl.when(jnp.logical_not(has_right))
    def _():
        out_ref[1] = jnp.zeros(out_ref.shape[1:], jnp.float32)

    @pl.when(has_right)
    def _():
        copy(0, col + 1).wait_send()

    @pl.when(has_left)
    def _():
        copy(1, col - 1).wait_send()


def main_kernel(
    half_ref, base_ref, moni_ref, halo_ref, coef_ref, knot_ref, shift_ref, normal_ref,
    stage, base, moni, timed, ebase, emoni, texp, tshift, tcorr, phi, model, flat,
):
    width = ebase.shape[1]
    rows = base.shape[1]
    lines = base_ref.shape[0] // (width * SUB)
    half = half_ref[0]
    take_two = (half >= 2).astype(jnp.float32)
    take_three = (half >= 3).astype(jnp.float32)
    lane = lax.broadcasted_iota(jnp.int32, (SUB, LANES), 1)
    block, tile = lane // WINLEN, lane % SUB
    not_first, not_last = block > 0, block < 3
    has_before, has_after = (tile > 0).astype(jnp.float32), (tile < SUB - 1).astype(jnp.float32)

    def trace_tile(which, ref, i, x):
        if x < HMAX:
            return halo_ref[0, edge_tile(which, x, i, lines), :]
        if x < HMAX + width:
            return ref[trace_rows(i, x - HMAX, width), :]
        if x < 2 * HMAX + width:
            return halo_ref[1, edge_tile(which, x - HMAX - width, i, lines), :]
        return jnp.zeros((SUB, LANES), jnp.float32)

    for which, (ref, wide, halo) in enumerate(((base_ref, base, TWIN), (moni_ref, moni, REACH))):
        for group in range(rows // 4):
            parts = [
                jnp.concatenate(
                    [trace_tile(which, ref, i, 4 * group + m) for i in range(lines)], axis=0
                )
                for m in range(4)
            ]
            turned = jnp.concatenate(swap_blocks(parts), axis=0).T
            stage[which, pl.ds(group * LANES, LANES), :] = turned
        for u in range(WINLEN):
            for part in range(rows // SUB):
                band = pl.ds(part * SUB, SUB)
                value = stage[which, pl.ds(part * SUB * WINLEN + u, SUB, stride=WINLEN), :]
                wide[halo + u, band, :] = value
                if u >= WINLEN - halo:
                    wide[halo + u - WINLEN, band, :] = jnp.where(
                        not_first, pltpu.roll(value, 32, 1), pltpu.roll(value, 33, 1) * has_before
                    )
                if u < halo:
                    wide[halo + u + WINLEN, band, :] = jnp.where(
                        not_last, pltpu.roll(value, 96, 1), pltpu.roll(value, 95, 1) * has_after
                    )

    def smooth(term, count, put):
        for part in range(rows // SUB):
            band = pl.ds(part * SUB, SUB)

            def keep(r, value, band=band):
                timed[r, band, :] = value

            box_sums(lambda r, band=band: term(r, band), count, keep)
        for r in range(count):
            for part in range(width // SUB):
                near = [timed[r, pl.ds(part * SUB + d, SUB), :] for d in range(2 * HMAX + 1)]
                value = near[3] + (near[2] + near[4])
                value = value + take_two * (near[1] + near[5])
                value = value + take_three * (near[0] + near[6])
                put(r, pl.ds(part * SUB, SUB), value)

    def base_square(r, band):
        value = base[r, band, :]
        return value * value

    def put_base(r, band, value):
        ebase[r, band, :] = value

    smooth(base_square, WINLEN, put_base)

    def moni_square(r, band):
        value = moni[r, band, :]
        return value * value

    def put_moni(r, band, value):
        emoni[r, band, :] = value

    smooth(moni_square, WINLEN + 2 * LAGS, put_moni)

    texp[...] = jnp.zeros_like(texp)
    tshift[...] = jnp.zeros_like(tshift)
    tcorr[...] = jnp.zeros_like(tcorr)

    @pl.loop(0, 2 * LAGS + 1)
    def _(lag):
        lag_value = (lag - LAGS).astype(jnp.float32)

        def product(r, band):
            return base[r, band, :] * moni[lag + r, band, :]

        def finish(r, band, value):
            energy = ebase[r, band, :] * emoni[lag + r, band, :] + EPSILON
            normed = value * lax.rsqrt(energy)
            weight = jnp.exp2(normed * (SHARPNESS * math.log2(math.e)))
            texp[r, band, :] += weight
            tshift[r, band, :] += lag_value * weight
            tcorr[r, band, :] += normed * weight

        smooth(product, WINLEN, finish)

    sample = lax.broadcasted_iota(jnp.int32, (WINLEN, LANES), 0).astype(jnp.float32)
    windows = knot_ref.shape[1]
    window = lax.broadcasted_iota(jnp.int32, (windows, LANES), 0)
    column = lax.broadcasted_iota(jnp.int32, (windows, LANES), 1)
    pick = (window == 4 * (column % SUB) + column // WINLEN).astype(jnp.float32)

    def spread(values):
        return lax.dot_general(
            values, pick, (((1,), (0,)), ((), ())),
            precision=lax.Precision.HIGHEST, preferred_element_type=jnp.float32,
        )

    starts = spread(knot_ref[...].astype(jnp.float32))
    for k in range(KW):
        phi[k] = spline((sample - starts[k : k + 1]) / KSTEP)
        model[k] = spread(coef_ref[k])

    for part in range(width // SUB):
        band = pl.ds(part * SUB, SUB)
        sums = [jnp.zeros((SUB, LANES), jnp.float32)] * TERMS
        for u in range(WINLEN):
            inverse = 1.0 / texp[u, band, :]
            observed = tshift[u, band, :] * inverse
            stage[0, pl.ds(part * SUB * WINLEN + u, SUB, stride=WINLEN), :] = observed
            conf = 0.5 + 0.5 * (tcorr[u, band, :] * inverse)
            basis = [phi[k, pl.ds(u, 1), :] for k in range(KW)]
            tau = model[0, band, :] * basis[0]
            for k in range(1, KW):
                tau = tau + model[k, band, :] * basis[k]
            weighted = conf * (observed - tau)
            for k in range(KW):
                sums[k] = sums[k] + weighted * basis[k]
            for place, (k, j) in enumerate(PAIRS):
                sums[KW + place] = sums[KW + place] + conf * (basis[k] * basis[j])
        for place in range(TERMS):
            value = sums[place]
            value = value + pltpu.roll(value, LANES - SUB, 1)
            value = value + pltpu.roll(value, LANES - 2 * SUB, 1)
            flat[pl.ds(place * width + part * SUB, SUB), :] = value
    spare = flat.shape[0] - TERMS * width
    if spare:
        flat[pl.ds(TERMS * width, spare), :] = jnp.zeros((spare, LANES), jnp.float32)
    turned = flat[...].T
    owners, share = normal_ref.shape[0], normal_ref.shape[1]
    for owner in range(owners):
        for j in range(share):
            window = owner * share + j
            place = (window % 4) * WINLEN + window // 4
            normal_ref[owner, j : j + 1] = turned[place : place + 1]
    for group in range(width // 4):
        back = stage[0, pl.ds(group * LANES, LANES), :].T
        parts = swap_blocks([back[WINLEN * m : WINLEN * (m + 1)] for m in range(4)])
        for m in range(4):
            for i in range(lines):
                shift_ref[trace_rows(i, 4 * group + m, width), :] = parts[m][SUB * i : SUB * (i + 1)]


def solve_small(matrix, target):
    lower = [[None] * KW for _ in range(KW)]
    for column in range(KW):
        pivot = matrix[column][column]
        for inner in range(column):
            pivot = pivot - lower[column][inner] * lower[column][inner]
        lower[column][column] = jnp.sqrt(pivot)
        for target_row in range(column + 1, KW):
            entry = matrix[target_row][column]
            for inner in range(column):
                entry = entry - lower[target_row][inner] * lower[column][inner]
            lower[target_row][column] = entry / lower[column][column]
    forward = []
    for column in range(KW):
        entry = target[column]
        for inner in range(column):
            entry = entry - lower[column][inner] * forward[inner]
        forward.append(entry / lower[column][column])
    backward = [None] * KW
    for column in range(KW - 1, -1, -1):
        entry = forward[column]
        for inner in range(column + 1, KW):
            entry = entry - lower[inner][column] * backward[inner]
        backward[column] = entry / lower[column][column]
    return backward


def owner_kernel(groups, slabs, width, damping, mine_ref, out_ref, held, send_sem, recv_sem):
    row, col = lax.axis_index("inl"), lax.axis_index("xl")
    each = slabs // groups
    target_row = col // each
    place = row * each + col % each
    barrier = pltpu.get_barrier_semaphore()
    for step in range(slabs):
        source_row, source_col = step // each, row * each + step % each

        @pl.when(jnp.logical_or(source_row != row, source_col != col))
        def _():
            pl.semaphore_signal(
                barrier, inc=1, device_id=(source_row, source_col), device_id_type=MESH_ID
            )

    @pl.when(target_row == row)
    def _():
        pl.semaphore_wait(barrier, slabs - 1)

    @pl.when(target_row != row)
    def _():
        pl.semaphore_wait(barrier, slabs)

    def send(step):
        return pltpu.make_async_remote_copy(
            src_ref=mine_ref.at[step],
            dst_ref=held.at[place],
            send_sem=send_sem.at[step],
            recv_sem=recv_sem.at[place],
            device_id=(target_row, step),
            device_id_type=MESH_ID,
        )

    def local():
        return pltpu.make_async_copy(mine_ref.at[col], held.at[place], recv_sem.at[place])

    for step in range(slabs):
        self_copy = jnp.logical_and(target_row == row, col == step)

        @pl.when(self_copy)
        def _():
            local().start()

        @pl.when(jnp.logical_not(self_copy))
        def _():
            send(step).start()

    for step in range(slabs):
        pltpu.make_async_copy(mine_ref.at[0], held.at[step], recv_sem.at[step]).wait()

    share = held.shape[1]
    totals = []
    for part in range(each):
        total = held[part]
        for group in range(1, groups):
            total = total + held[group * each + part]
        totals.append(total)
    total = jnp.concatenate(totals, axis=0)

    def term(number):
        return total[:, number * width : (number + 1) * width]

    matrix = [[None] * KW for _ in range(KW)]
    for number, (k, j) in enumerate(PAIRS):
        matrix[k][j] = term(KW + number) + (damping if k == j else 0.0)
    delta = solve_small(matrix, [term(k) for k in range(KW)])
    for k in range(KW):
        for part in range(each):
            value = delta[k][part * share : (part + 1) * share]
            out_ref[k, :, pl.ds(part * width, width)] = value

    for step in range(slabs):
        self_copy = jnp.logical_and(target_row == row, col == step)

        @pl.when(jnp.logical_not(self_copy))
        def _():
            send(step).wait_send()


def as_rows(block):
    lines, width, samples = block.shape
    tiles = block.reshape(lines, width // SUB, SUB, samples // LANES, LANES)
    return tiles.transpose(0, 1, 3, 2, 4).reshape(-1, LANES)


def from_rows(flat, lines, width, samples):
    tiles = flat.reshape(lines, width // SUB, samples // LANES, SUB, LANES)
    return tiles.transpose(0, 1, 3, 2, 4).reshape(lines, width, samples)


def per_device(baseline, monitor, shift_model, knot_start, half_width):
    lines, width, samples = baseline.shape
    windows = samples // WINLEN
    groups, slabs = lax.axis_size("inl"), lax.axis_size("xl")
    share, each = windows // slabs, slabs // groups
    rows = -(-(width + 2 * HMAX) // SUB) * SUB
    packed = -(-(TERMS * width) // LANES) * LANES
    block = (WINLEN, width, LANES)
    f32 = jnp.float32
    whole = pl.BlockSpec(memory_space=pltpu.VMEM)
    base_rows, moni_rows = as_rows(baseline), as_rows(monitor)
    edges = (2, 2 * HMAX * lines * SUB, LANES)
    halo = pl.pallas_call(
        functools.partial(halo_kernel, width),
        out_shape=jax.ShapeDtypeStruct(edges, f32),
        in_specs=[whole, whole],
        out_specs=whole,
        scratch_shapes=[
            pltpu.VMEM(edges, f32),
            pltpu.VMEM(edges, f32),
            pltpu.SemaphoreType.DMA((2,)),
            pltpu.SemaphoreType.DMA((2,)),
        ],
        compiler_params=pltpu.CompilerParams(collective_id=1, has_side_effects=True),
        name="halo",
    )(base_rows, moni_rows)
    shift, normal = pl.pallas_call(
        main_kernel,
        out_shape=(
            jax.ShapeDtypeStruct(base_rows.shape, f32),
            jax.ShapeDtypeStruct((slabs, share, packed), f32),
        ),
        in_specs=[pl.BlockSpec(memory_space=pltpu.SMEM)] + [whole] * 5,
        out_specs=(whole, whole),
        scratch_shapes=[
            pltpu.VMEM((2, rows * WINLEN, LANES), f32),
            pltpu.VMEM((WINLEN + 2 * TWIN, rows, LANES), f32),
            pltpu.VMEM((WINLEN + 2 * REACH + 2, rows, LANES), f32),
            pltpu.VMEM((WINLEN + 2 * LAGS, rows, LANES), f32),
            pltpu.VMEM(block, f32),
            pltpu.VMEM((WINLEN + 2 * LAGS, width, LANES), f32),
            pltpu.VMEM(block, f32),
            pltpu.VMEM(block, f32),
            pltpu.VMEM(block, f32),
            pltpu.VMEM((KW, WINLEN, LANES), f32),
            pltpu.VMEM((KW, width, LANES), f32),
            pltpu.VMEM((packed, LANES), f32),
        ],
        compiler_params=pltpu.CompilerParams(vmem_limit_bytes=32 * 1024 * 1024),
        name="lags",
    )(half_width, base_rows, moni_rows, halo, shift_model.transpose(0, 2, 1), knot_start.T)
    shift_obs = from_rows(shift, lines, width, samples)
    delta = pl.pallas_call(
        functools.partial(owner_kernel, groups, slabs, width, DAMPING * lines * groups),
        out_shape=jax.ShapeDtypeStruct((KW, share, each * width), f32),
        in_specs=[whole],
        out_specs=whole,
        scratch_shapes=[
            pltpu.VMEM((slabs, share, packed), f32),
            pltpu.SemaphoreType.DMA((slabs,)),
            pltpu.SemaphoreType.DMA((slabs,)),
        ],
        compiler_params=pltpu.CompilerParams(collective_id=0, has_side_effects=True),
        name="owners",
    )(normal)
    return (shift_obs, delta)


def solution(mesh):
    in_specs = (P("inl", "xl", None), P("inl", "xl", None), P(None, None, "xl"), P(), P("xl"))
    out_specs = (P("inl", "xl", None), P(None, "xl", "inl"))
    return jax.shard_map(
        per_device, mesh=mesh, in_specs=in_specs, out_specs=out_specs, check_vma=False
    )
```

```python
import functools
import math

import jax
import jax.numpy as jnp
from jax import lax
from jax.experimental import pallas as pl
from jax.experimental.pallas import tpu as pltpu
from jax.sharding import PartitionSpec as P

LAGS = 15
TWIN = 12
HMAX = 3
WINLEN = 32
KW = 4
KSTEP = 8
EPSILON = 1e-06
SHARPNESS = 6.0
DAMPING = 0.5

LANES = 128
SUB = 8
REACH = LAGS + TWIN
PAIRS = [(k, j) for k in range(KW) for j in range(k + 1)]
TERMS = KW + len(PAIRS)
MESH_ID = pl.DeviceIdType.MESH


def spline(offset):
    square = offset * offset
    cubed = square * offset
    piece_one = cubed / 6.0
    piece_two = (-3.0 * cubed + 12.0 * square - 12.0 * offset + 4.0) / 6.0
    piece_three = (3.0 * cubed - 24.0 * square + 60.0 * offset - 44.0) / 6.0
    remain = 4.0 - offset
    piece_four = remain * remain * remain / 6.0
    result = jnp.where(offset < 4.0, piece_four, 0.0 * offset)
    result = jnp.where(offset < 3.0, piece_three, result)
    result = jnp.where(offset < 2.0, piece_two, result)
    result = jnp.where(offset < 1.0, piece_one, result)
    return jnp.where(offset < 0.0, 0.0 * offset, result)


def box_sums(term, count, put):
    outs = -(-count // SUB)
    terms = {}

    def block(number):
        if number not in terms:
            terms[number] = [term(number * SUB + j) for j in range(SUB)]
        return terms[number]

    totals = {}
    suffixes = {}

    def total(number):
        if number not in totals:
            vals = block(number)
            while len(vals) > 1:
                vals = [vals[2 * j] + vals[2 * j + 1] for j in range(len(vals) // 2)]
            totals[number] = vals[0]
        return totals[number]

    def suffix(number):
        if number not in suffixes:
            vals = list(block(number))
            for j in range(SUB - 2, -1, -1):
                vals[j] = vals[j] + vals[j + 1]
            suffixes[number] = vals
            totals[number] = vals[0]
        return suffixes[number]

    for number in range(outs):
        tail = suffix(number)
        if number + 1 < outs:
            suffix(number + 1)
        if number + 2 < outs:
            suffix(number + 2)
        run = total(number + 1) + total(number + 2)
        for j in range(SUB):
            if number * SUB + j < count:
                position = (number + 3) * SUB + j
                if number + 3 in terms:
                    value = terms[number + 3][j]
                elif number + 3 < outs + 2:
                    value = block(number + 3)[j]
                else:
                    value = term(position)
                run = run + value
                put(number * SUB + j, tail[j] + run)


def trace_rows(i, x, width):
    return pl.ds((i * (width // SUB) + x // SUB) * SUB * SUB + x % SUB, SUB, stride=SUB)


def edge_tile(which, j, i, lines):
    return pl.ds(((which * HMAX + j) * lines + i) * SUB, SUB)


def swap_blocks(parts):
    block = lax.broadcasted_iota(jnp.int32, parts[0].shape, 1) // WINLEN
    low, even = block < 2, block % 2 == 0
    w, x, y, z = parts
    w, y = jnp.where(low, w, pltpu.roll(y, 64, 1)), jnp.where(low, pltpu.roll(w, 64, 1), y)
    x, z = jnp.where(low, x, pltpu.roll(z, 64, 1)), jnp.where(low, pltpu.roll(x, 64, 1), z)
    w, x = jnp.where(even, w, pltpu.roll(x, 32, 1)), jnp.where(even, pltpu.roll(w, 96, 1), x)
    y, z = jnp.where(even, y, pltpu.roll(z, 32, 1)), jnp.where(even, pltpu.roll(y, 96, 1), z)
    return [w, x, y, z]


def halo_kernel(width, base_ref, moni_ref, out_ref, edge, held, send_sem, recv_sem):
    row, col = lax.axis_index("inl"), lax.axis_index("xl")
    last = lax.axis_size("xl") - 1
    lines = base_ref.shape[0] // (width * SUB)
    barrier = pltpu.get_barrier_semaphore()
    has_left, has_right = col > 0, col < last

    @pl.when(has_left)
    def _():
        pl.semaphore_signal(barrier, inc=1, device_id=(row, col - 1), device_id_type=MESH_ID)

    @pl.when(has_right)
    def _():
        pl.semaphore_signal(barrier, inc=1, device_id=(row, col + 1), device_id_type=MESH_ID)

    for side, first in ((0, width - HMAX), (1, 0)):
        for which, ref in enumerate((base_ref, moni_ref)):
            for j in range(HMAX):
                for i in range(lines):
                    value = ref[trace_rows(i, first + j, width), :]
                    edge[side, edge_tile(which, j, i, lines), :] = value

    @pl.when(jnp.logical_and(has_left, has_right))
    def _():
        pl.semaphore_wait(barrier, 2)

    @pl.when(jnp.logical_not(jnp.logical_and(has_left, has_right)))
    def _():
        pl.semaphore_wait(barrier, 1)

    def copy(side, target):
        return pltpu.make_async_remote_copy(
            src_ref=edge.at[side],
            dst_ref=held.at[side],
            send_sem=send_sem.at[side],
            recv_sem=recv_sem.at[side],
            device_id=(row, target),
            device_id_type=MESH_ID,
        )

    @pl.when(has_right)
    def _():
        copy(0, col + 1).start()

    @pl.when(has_left)
    def _():
        copy(1, col - 1).start()

    @pl.when(has_left)
    def _():
        pltpu.make_async_copy(edge.at[0], held.at[0], recv_sem.at[0]).wait()
        out_ref[0] = held[0]

    @pl.when(jnp.logical_not(has_left))
    def _():
        out_ref[0] = jnp.zeros(out_ref.shape[1:], jnp.float32)

    @pl.when(has_right)
    def _():
        pltpu.make_async_copy(edge.at[1], held.at[1], recv_sem.at[1]).wait()
        out_ref[1] = held[1]

    @pl.when(jnp.logical_not(has_right))
    def _():
        out_ref[1] = jnp.zeros(out_ref.shape[1:], jnp.float32)

    @pl.when(has_right)
    def _():
        copy(0, col + 1).wait_send()

    @pl.when(has_left)
    def _():
        copy(1, col - 1).wait_send()


def main_kernel(
    half_ref, base_ref, moni_ref, halo_ref, coef_ref, knot_ref, shift_ref, normal_ref,
    stage, base, moni, timed, ebase, emoni, texp, tshift, tcorr, phi, model, flat,
):
    width = ebase.shape[1]
    rows = base.shape[1]
    lines = base_ref.shape[0] // (width * SUB)
    half = half_ref[0]
    take_two = (half >= 2).astype(jnp.float32)
    take_three = (half >= 3).astype(jnp.float32)
    lane = lax.broadcasted_iota(jnp.int32, (SUB, LANES), 1)
    block, tile = lane // WINLEN, lane % SUB
    not_first, not_last = block > 0, block < 3
    has_before, has_after = (tile > 0).astype(jnp.float32), (tile < SUB - 1).astype(jnp.float32)

    def trace_tile(which, ref, i, x):
        if x < HMAX:
            return halo_ref[0, edge_tile(which, x, i, lines), :]
        if x < HMAX + width:
            return ref[trace_rows(i, x - HMAX, width), :]
        if x < 2 * HMAX + width:
            return halo_ref[1, edge_tile(which, x - HMAX - width, i, lines), :]
        return jnp.zeros((SUB, LANES), jnp.float32)

    for which, (ref, wide, halo) in enumerate(((base_ref, base, TWIN), (moni_ref, moni, REACH))):
        for group in range(rows // 4):
            parts = [
                jnp.concatenate(
                    [trace_tile(which, ref, i, 4 * group + m) for i in range(lines)], axis=0
                )
                for m in range(4)
            ]
            turned = jnp.concatenate(swap_blocks(parts), axis=0).T
            stage[which, pl.ds(group * LANES, LANES), :] = turned
        for u in range(WINLEN):
            for part in range(rows // SUB):
                band = pl.ds(part * SUB, SUB)
                value = stage[which, pl.ds(part * SUB * WINLEN + u, SUB, stride=WINLEN), :]
                wide[halo + u, band, :] = value
                if u >= WINLEN - halo:
                    wide[halo + u - WINLEN, band, :] = jnp.where(
                        not_first, pltpu.roll(value, 32, 1), pltpu.roll(value, 33, 1) * has_before
                    )
                if u < halo:
                    wide[halo + u + WINLEN, band, :] = jnp.where(
                        not_last, pltpu.roll(value, 96, 1), pltpu.roll(value, 95, 1) * has_after
                    )

    def smooth(term, count, put):
        for part in range(rows // SUB):
            band = pl.ds(part * SUB, SUB)

            def keep(r, value, band=band):
                timed[r, band, :] = value

            box_sums(lambda r, band=band: term(r, band), count, keep)
        for r in range(count):
            for part in range(width // SUB):
                near = [timed[r, pl.ds(part * SUB + d, SUB), :] for d in range(2 * HMAX + 1)]
                value = near[3] + (near[2] + near[4])
                value = value + take_two * (near[1] + near[5])
                value = value + take_three * (near[0] + near[6])
                put(r, pl.ds(part * SUB, SUB), value)

    def base_square(r, band):
        value = base[r, band, :]
        return value * value

    def put_base(r, band, value):
        ebase[r, band, :] = value

    smooth(base_square, WINLEN, put_base)

    def moni_square(r, band):
        value = moni[r, band, :]
        return value * value

    def put_moni(r, band, value):
        emoni[r, band, :] = value

    smooth(moni_square, WINLEN + 2 * LAGS, put_moni)

    texp[...] = jnp.zeros_like(texp)
    tshift[...] = jnp.zeros_like(tshift)
    tcorr[...] = jnp.zeros_like(tcorr)

    @pl.loop(0, 2 * LAGS + 1)
    def _(lag):
        lag_value = (lag - LAGS).astype(jnp.float32)

        def product(r, band):
            return base[r, band, :] * moni[lag + r, band, :]

        def finish(r, band, value):
            energy = ebase[r, band, :] * emoni[lag + r, band, :] + EPSILON
            normed = value * lax.rsqrt(energy)
            weight = jnp.exp2(normed * (SHARPNESS * math.log2(math.e)))
            texp[r, band, :] += weight
            tshift[r, band, :] += lag_value * weight
            tcorr[r, band, :] += normed * weight

        smooth(product, WINLEN, finish)

    sample = lax.broadcasted_iota(jnp.int32, (WINLEN, LANES), 0).astype(jnp.float32)
    windows = knot_ref.shape[1]
    window = lax.broadcasted_iota(jnp.int32, (windows, LANES), 0)
    column = lax.broadcasted_iota(jnp.int32, (windows, LANES), 1)
    pick = (window == 4 * (column % SUB) + column // WINLEN).astype(jnp.float32)

    def spread(values):
        return lax.dot_general(
            values, pick, (((1,), (0,)), ((), ())),
            precision=lax.Precision.HIGHEST, preferred_element_type=jnp.float32,
        )

    starts = spread(knot_ref[...].astype(jnp.float32))
    for k in range(KW):
        phi[k] = spline((sample - starts[k : k + 1]) / KSTEP)
        model[k] = spread(coef_ref[k])

    for part in range(width // SUB):
        band = pl.ds(part * SUB, SUB)
        sums = [jnp.zeros((SUB, LANES), jnp.float32)] * TERMS
        for u in range(WINLEN):
            inverse = 1.0 / texp[u, band, :]
            observed = tshift[u, band, :] * inverse
            stage[0, pl.ds(part * SUB * WINLEN + u, SUB, stride=WINLEN), :] = observed
            conf = 0.5 + 0.5 * (tcorr[u, band, :] * inverse)
            basis = [phi[k, pl.ds(u, 1), :] for k in range(KW)]
            tau = model[0, band, :] * basis[0]
            for k in range(1, KW):
                tau = tau + model[k, band, :] * basis[k]
            weighted = conf * (observed - tau)
            for k in range(KW):
                sums[k] = sums[k] + weighted * basis[k]
            for place, (k, j) in enumerate(PAIRS):
                sums[KW + place] = sums[KW + place] + conf * (basis[k] * basis[j])
        for place in range(TERMS):
            value = sums[place]
            value = value + pltpu.roll(value, LANES - SUB, 1)
            value = value + pltpu.roll(value, LANES - 2 * SUB, 1)
            flat[pl.ds(place * width + part * SUB, SUB), :] = value
    spare = flat.shape[0] - TERMS * width
    if spare:
        flat[pl.ds(TERMS * width, spare), :] = jnp.zeros((spare, LANES), jnp.float32)
    turned = flat[...].T
    owners, share = normal_ref.shape[0], normal_ref.shape[1]
    for owner in range(owners):
        for j in range(share):
            window = owner * share + j
            place = (window % 4) * WINLEN + window // 4
            normal_ref[owner, j : j + 1] = turned[place : place + 1]
    for group in range(width // 4):
        back = stage[0, pl.ds(group * LANES, LANES), :].T
        parts = swap_blocks([back[WINLEN * m : WINLEN * (m + 1)] for m in range(4)])
        for m in range(4):
            for i in range(lines):
                shift_ref[trace_rows(i, 4 * group + m, width), :] = parts[m][SUB * i : SUB * (i + 1)]


def solve_small(matrix, target):
    lower = [[None] * KW for _ in range(KW)]
    for column in range(KW):
        pivot = matrix[column][column]
        for inner in range(column):
            pivot = pivot - lower[column][inner] * lower[column][inner]
        lower[column][column] = jnp.sqrt(pivot)
        for target_row in range(column + 1, KW):
            entry = matrix[target_row][column]
            for inner in range(column):
                entry = entry - lower[target_row][inner] * lower[column][inner]
            lower[target_row][column] = entry / lower[column][column]
    forward = []
    for column in range(KW):
        entry = target[column]
        for inner in range(column):
            entry = entry - lower[column][inner] * forward[inner]
        forward.append(entry / lower[column][column])
    backward = [None] * KW
    for column in range(KW - 1, -1, -1):
        entry = forward[column]
        for inner in range(column + 1, KW):
            entry = entry - lower[inner][column] * backward[inner]
        backward[column] = entry / lower[column][column]
    return backward


def owner_kernel(groups, slabs, width, damping, mine_ref, out_ref, held, send_sem, recv_sem):
    row, col = lax.axis_index("inl"), lax.axis_index("xl")
    each = slabs // groups
    target_row = col // each
    place = row * each + col % each
    barrier = pltpu.get_barrier_semaphore()
    for step in range(slabs):
        source_row, source_col = step // each, row * each + step % each

        @pl.when(jnp.logical_or(source_row != row, source_col != col))
        def _():
            pl.semaphore_signal(
                barrier, inc=1, device_id=(source_row, source_col), device_id_type=MESH_ID
            )

    @pl.when(target_row == row)
    def _():
        pl.semaphore_wait(barrier, slabs - 1)

    @pl.when(target_row != row)
    def _():
        pl.semaphore_wait(barrier, slabs)

    def send(step):
        return pltpu.make_async_remote_copy(
            src_ref=mine_ref.at[step],
            dst_ref=held.at[place],
            send_sem=send_sem.at[step],
            recv_sem=recv_sem.at[place],
            device_id=(target_row, step),
            device_id_type=MESH_ID,
        )

    def local():
        return pltpu.make_async_copy(mine_ref.at[col], held.at[place], recv_sem.at[place])

    for step in range(slabs):
        self_copy = jnp.logical_and(target_row == row, col == step)

        @pl.when(self_copy)
        def _():
            local().start()

        @pl.when(jnp.logical_not(self_copy))
        def _():
            send(step).start()

    for step in range(slabs):
        pltpu.make_async_copy(mine_ref.at[0], held.at[step], recv_sem.at[step]).wait()

    share = held.shape[1]
    totals = []
    for part in range(each):
        total = held[part]
        for group in range(1, groups):
            total = total + held[group * each + part]
        totals.append(total)
    total = jnp.concatenate(totals, axis=0)

    def term(number):
        return total[:, number * width : (number + 1) * width]

    matrix = [[None] * KW for _ in range(KW)]
    for number, (k, j) in enumerate(PAIRS):
        matrix[k][j] = term(KW + number) + (damping if k == j else 0.0)
    delta = solve_small(matrix, [term(k) for k in range(KW)])
    for k in range(KW):
        for part in range(each):
            value = delta[k][part * share : (part + 1) * share]
            out_ref[k, :, pl.ds(part * width, width)] = value

    for step in range(slabs):
        self_copy = jnp.logical_and(target_row == row, col == step)

        @pl.when(jnp.logical_not(self_copy))
        def _():
            send(step).wait_send()


def as_rows(block):
    lines, width, samples = block.shape
    tiles = block.reshape(lines, width // SUB, SUB, samples // LANES, LANES)
    return tiles.transpose(0, 1, 3, 2, 4).reshape(-1, LANES)


def from_rows(flat, lines, width, samples):
    tiles = flat.reshape(lines, width // SUB, samples // LANES, SUB, LANES)
    return tiles.transpose(0, 1, 3, 2, 4).reshape(lines, width, samples)


def per_device(baseline, monitor, shift_model, knot_start, half_width):
    lines, width, samples = baseline.shape
    windows = samples // WINLEN
    groups, slabs = lax.axis_size("inl"), lax.axis_size("xl")
    share, each = windows // slabs, slabs // groups
    rows = -(-(width + 2 * HMAX) // SUB) * SUB
    packed = -(-(TERMS * width) // LANES) * LANES
    block = (WINLEN, width, LANES)
    f32 = jnp.float32
    whole = pl.BlockSpec(memory_space=pltpu.VMEM)
    base_rows, moni_rows = as_rows(baseline), as_rows(monitor)
    edges = (2, 2 * HMAX * lines * SUB, LANES)
    halo = pl.pallas_call(
        functools.partial(halo_kernel, width),
        out_shape=jax.ShapeDtypeStruct(edges, f32),
        in_specs=[whole, whole],
        out_specs=whole,
        scratch_shapes=[
            pltpu.VMEM(edges, f32),
            pltpu.VMEM(edges, f32),
            pltpu.SemaphoreType.DMA((2,)),
            pltpu.SemaphoreType.DMA((2,)),
        ],
        compiler_params=pltpu.CompilerParams(collective_id=1, has_side_effects=True, vmem_limit_bytes=8 * 1024 * 1024),
        name="halo",
    )(base_rows, moni_rows)
    shift, normal = pl.pallas_call(
        main_kernel,
        out_shape=(
            jax.ShapeDtypeStruct(base_rows.shape, f32),
            jax.ShapeDtypeStruct((slabs, share, packed), f32),
        ),
        in_specs=[pl.BlockSpec(memory_space=pltpu.SMEM)] + [whole] * 5,
        out_specs=(whole, whole),
        scratch_shapes=[
            pltpu.VMEM((2, rows * WINLEN, LANES), f32),
            pltpu.VMEM((WINLEN + 2 * TWIN, rows, LANES), f32),
            pltpu.VMEM((WINLEN + 2 * REACH + 2, rows, LANES), f32),
            pltpu.VMEM((WINLEN + 2 * LAGS, rows, LANES), f32),
            pltpu.VMEM(block, f32),
            pltpu.VMEM((WINLEN + 2 * LAGS, width, LANES), f32),
            pltpu.VMEM(block, f32),
            pltpu.VMEM(block, f32),
            pltpu.VMEM(block, f32),
            pltpu.VMEM((KW, WINLEN, LANES), f32),
            pltpu.VMEM((KW, width, LANES), f32),
            pltpu.VMEM((packed, LANES), f32),
        ],
        compiler_params=pltpu.CompilerParams(vmem_limit_bytes=32 * 1024 * 1024),
        name="lags",
    )(half_width, base_rows, moni_rows, halo, shift_model.transpose(0, 2, 1), knot_start.T)
    shift_obs = from_rows(shift, lines, width, samples)
    delta = pl.pallas_call(
        functools.partial(owner_kernel, groups, slabs, width, DAMPING * lines * groups),
        out_shape=jax.ShapeDtypeStruct((KW, share, each * width), f32),
        in_specs=[whole],
        out_specs=whole,
        scratch_shapes=[
            pltpu.VMEM((slabs, share, packed), f32),
            pltpu.SemaphoreType.DMA((slabs,)),
            pltpu.SemaphoreType.DMA((slabs,)),
        ],
        compiler_params=pltpu.CompilerParams(collective_id=0, has_side_effects=True, vmem_limit_bytes=8 * 1024 * 1024),
        name="owners",
    )(normal)
    return (shift_obs, delta)


def solution(mesh):
    in_specs = (P("inl", "xl", None), P("inl", "xl", None), P(None, None, "xl"), P(), P("xl"))
    out_specs = (P("inl", "xl", None), P(None, "xl", "inl"))
    return jax.shard_map(
        per_device, mesh=mesh, in_specs=in_specs, out_specs=out_specs, check_vma=False
    )
```
